32 devices in a mesh: dom: 8 (over y, x, core), feat: 4 (over z).
Axes of the slice: x: 2, y: 2, z: 4, core: 2. Of those that a mesh axis runs over, the one named last changes fastest.
Arguments:
- node_x: bfloat16 [2048, 256], P('dom', 'feat'), may hold values from -24 to 24, as said below
- cotangent: bfloat16 [2048, 256], P('dom', 'feat'), may hold values from -6 to 6
- assign: int32 [2048], P('dom'), may hold values from 0 to 4095
- part_sizes: int32 [8], P('dom'), may hold values from 64 to 256, as said below
- w_query: bfloat16 [256, 256], replicated, may hold values from -0.375 to 0.375
- w_key: bfloat16 [256, 256], replicated, may hold values from -1.5 to 1.5
- w_value: bfloat16 [256, 256], replicated, may hold values from -0.75 to 0.75
- w_out: bfloat16 [256, 256], replicated, may hold values from -0.375 to 0.375
Outputs:
- result_out: bfloat16 [2048, 256], P('dom', 'feat')
- grad_x: bfloat16 [2048, 256], P('dom', 'feat')
The draws below stay inside these ranges and needn't reach their ends.
Inputs may be any that keep to these rules, and one draw needn't show every extreme that they name: `node_x`: node features; in the hidden draw rows differ in scale. Partition p holds live nodes in its first part_sizes[p] slots; in every draw some partition is full.
All inputs are finite; a program needn't handle non-finite values.
Results may differ from the reference program's by a relative error of at most 0.006.
The reference program's roundings to bfloat16 on the way (of `cent`, `query`, `probs_low`, `attended`, `g_attended`, `g_scores` and `g_query`) count: a program that leaves them out, or rounds other values in their place, can miss the bound.
Values may be sent and summed in bfloat16 or wider, within the bound.
A program may use at most 64 MiB of HBM per device.

```python
import math
import jax
import jax.numpy as jnp
import numpy as np
from jax import lax

D = 256
HEADS = 4
CENTROIDS = 4096
ROWS_DEV = 256
GROUPS = 8
NODES = 2048
N_DOM = 8


def draw_node_x(key, part):
    normals = jax.random.normal(jax.random.fold_in(key, 5), (NODES, D), jnp.float32)
    normals = jnp.clip(normals, -6.0, 6.0)
    return normals.astype(jnp.bfloat16)


def draw_part_sizes(key, part):
    key_one, key_two = jax.random.split(jax.random.fold_in(key, 11))
    live_counts = jax.random.randint(key_one, (GROUPS,), ROWS_DEV // 4, ROWS_DEV + 1)
    full_index = jax.random.randint(key_two, (), 0, GROUPS)
    places = jnp.arange(GROUPS, dtype=jnp.int32)
    return jnp.where(places == full_index, ROWS_DEV, live_counts).astype(jnp.int32)


def with_ends(values, stream_key, smallest, largest):
    longest = values.shape.index(max(values.shape))
    spots = []
    for shift in (0, 1):
        where = [jax.random.randint(jax.random.fold_in(stream_key, axis), (), 0, length) for axis, length in enumerate(values.shape)]
        where[longest] = (where[longest] + shift) % values.shape[longest]
        spots.append(tuple(where))
    return values.at[spots[0]].set(smallest).at[spots[1]].set(largest)


def levels(rng, dims, shards, low, high):
    def one(axis_at, parts):
        draws = jax.random.uniform(jax.random.fold_in(jax.random.fold_in(rng, 6), axis_at), (parts,), jnp.float32, low / len(shards), high / len(shards))
        return jnp.repeat(jnp.exp(draws), dims[axis_at] // parts).reshape((-1,) + (1,) * (len(dims) - axis_at - 1))

    gain = one(*shards[0])
    for cut in shards[1:]:
        gain = gain * one(*cut)
    return gain


def rank_table(count, lean):
    loads = [(1 << 20) // math.isqrt(standing ** lean) + 1 for standing in range(1, count + 1)]
    scale = 1 + sum(loads) // (1 << 30)
    return np.cumsum(np.array([max(1, weight // scale) for weight in loads]))


def skewed_ids(stream_key, dims, count, slope):
    listing = rank_table(count, slope)
    ticket = jax.random.randint(jax.random.fold_in(stream_key, 1), dims, 0, int(listing[count - 1]))
    standing = jnp.searchsorted(jnp.asarray(listing, jnp.int32), ticket, side="right")
    return jax.random.permutation(jax.random.fold_in(stream_key, 2), count)[standing].astype(jnp.int32)


def normal_values(rng, extent, width, bound, cuts=(), kind=jnp.bfloat16):
    values = width * jax.random.normal(rng, extent, jnp.float32)
    if cuts:
        values = values * levels(rng, extent, cuts, -0.22, 0.18)
    return jnp.clip(values, -bound, bound).astype(kind)


def setup_inputs(seed: int = 0) -> dict:
    arg_keys = jax.random.split(jax.random.key(seed), 9)
    return {
        "node_x": draw_node_x(jax.random.fold_in(arg_keys[8], 71), 0),
        "cotangent": normal_values(arg_keys[1], (NODES, D), 1.0, 6.0, ((0, 8), (1, 4))),
        "assign": with_ends(skewed_ids(arg_keys[2], (NODES,), CENTROIDS, 1), jax.random.fold_in(arg_keys[2], 3), 0, CENTROIDS - 1).astype(jnp.int32),
        "part_sizes": draw_part_sizes(jax.random.fold_in(arg_keys[8], 71), 0),
        "w_query": normal_values(arg_keys[4], (D, D), D ** -0.5, 0.375),
        "w_key": normal_values(arg_keys[5], (D, D), (D // 16) ** -0.5, 1.5),
        "w_value": normal_values(arg_keys[6], (D, D), (D // 4) ** -0.5, 0.75),
        "w_out": normal_values(arg_keys[7], (D, D), D ** -0.5, 0.375),
    }


def reference(node_x, cotangent, assign, part_sizes, w_query, w_key, w_value, w_out):
    node_total = node_x.shape[0]
    row_count = node_total // N_DOM
    head_width = D // HEADS
    inv_root = 1.0 / (head_width ** 0.5)
    positions = jnp.arange(node_total, dtype=jnp.int32)
    alive_rows = (positions % row_count < part_sizes[positions // row_count]).astype(jnp.float32)
    counts = jax.ops.segment_sum(alive_rows, assign, CENTROIDS)
    cent_sums = jax.ops.segment_sum(alive_rows[:, None] * node_x.astype(jnp.float32), assign, CENTROIDS)
    cent = (cent_sums / (counts + 1.0)[:, None]).astype(jnp.bfloat16)
    keys = jnp.dot(cent, w_key, preferred_element_type=jnp.float32).astype(jnp.bfloat16)
    values = jnp.dot(cent, w_value, preferred_element_type=jnp.float32).astype(jnp.bfloat16)
    query = jnp.dot(node_x, w_query, preferred_element_type=jnp.float32).astype(jnp.bfloat16)
    g_attended = (alive_rows[:, None] * lax.dot_general(cotangent, w_out, (((1,), (1,)), ((), ())), preferred_element_type=jnp.float32)).astype(jnp.bfloat16)
    block_rows = min(512, node_total)
    block_count = node_total // block_rows

    def attend(running, block_pair):
        query_block, grad_block = block_pair
        att_parts = []
        gq_parts = []
        kv_parts = []
        for head_index in range(HEADS):
            offset = head_index * head_width
            query_head = query_block[:, offset:offset + head_width]
            grad_head = grad_block[:, offset:offset + head_width]
            keys_head = keys[:, offset:offset + head_width]
            values_head = values[:, offset:offset + head_width]
            scores = lax.dot_general(query_head, keys_head, (((1,), (1,)), ((), ())), preferred_element_type=jnp.float32) * inv_root
            probs = jax.nn.softmax(scores, axis=1)
            probs_low = probs.astype(jnp.bfloat16)
            att_parts.append(jnp.dot(probs_low, values_head, preferred_element_type=jnp.float32).astype(jnp.bfloat16))
            g_probs = lax.dot_general(grad_head, values_head, (((1,), (1,)), ((), ())), preferred_element_type=jnp.float32)
            row_delta = jnp.sum(probs * g_probs, axis=1, keepdims=True)
            g_scores = (probs * (g_probs - row_delta) * inv_root).astype(jnp.bfloat16)
            gq_parts.append(jnp.dot(g_scores, keys_head, preferred_element_type=jnp.float32).astype(jnp.bfloat16))
            key_grad = lax.dot_general(g_scores, query_head, (((0,), (0,)), ((), ())), preferred_element_type=jnp.float32)
            value_grad = lax.dot_general(probs_low, grad_head, (((0,), (0,)), ((), ())), preferred_element_type=jnp.float32)
            kv_parts.append(jnp.stack([key_grad, value_grad]))
        return running + jnp.concatenate(kv_parts, axis=2), (jnp.concatenate(att_parts, axis=1), jnp.concatenate(gq_parts, axis=1))

    start_grads = jnp.zeros((2, CENTROIDS, D), jnp.float32)
    kv_total, outputs = lax.scan(attend, start_grads, (query.reshape(block_count, block_rows, D), g_attended.reshape(block_count, block_rows, D)))
    attended = outputs[0].reshape(node_total, D)
    g_query = outputs[1].reshape(node_total, D)
    result_out = (alive_rows[:, None] * jnp.dot(attended, w_out, preferred_element_type=jnp.float32)).astype(jnp.bfloat16)
    key_grad_low = kv_total[0].astype(jnp.bfloat16)
    value_grad_low = kv_total[1].astype(jnp.bfloat16)
    cent_grad = lax.dot_general(key_grad_low, w_key, (((1,), (1,)), ((), ())), preferred_element_type=jnp.float32)
    cent_grad = cent_grad + lax.dot_general(value_grad_low, w_value, (((1,), (1,)), ((), ())), preferred_element_type=jnp.float32)
    cent_grad = cent_grad / (counts + 1.0)[:, None]
    from_query = lax.dot_general(g_query, w_query, (((1,), (1,)), ((), ())), preferred_element_type=jnp.float32)
    grad_x = (from_query + alive_rows[:, None] * jnp.take(cent_grad, assign, axis=0)).astype(jnp.bfloat16)
    return result_out, grad_x
```

```python
import functools

import jax
import jax.numpy as jnp
from jax import lax
from jax.experimental import pallas as pl
from jax.experimental.pallas import tpu as pltpu
from jax.sharding import PartitionSpec as P

HEADS = 4
CENTROIDS = 4096
MESH = pl.DeviceIdType.MESH
BF = jnp.bfloat16
F32 = jnp.float32


def dot(left, right, left_dim, right_dim):
    return lax.dot_general(
        left, right, (((left_dim,), (right_dim,)), ((), ())), preferred_element_type=F32
    )


def kernel(
    n_dom,
    n_feat,
    x_ref,
    cot_ref,
    assign_ref,
    size_ref,
    wq_ref,
    wk_ref,
    wv_ref,
    wo_ref,
    out_ref,
    gx_ref,
    xp,
    am,
    xc,
    ct,
    rep,
    kvb,
    qg,
    st,
    gsend,
    grecv,
    aqs,
    aqr,
    kg,
    aq,
    e_buf,
    g_buf,
    xp_sem,
    am_sem,
    xc_sem,
    ct_sem,
    rep_sem,
    kv_sem,
    qg_sem,
    st_sem,
    gr_sem,
    ap_sem,
    kg_sem,
    aq_sem,
):
    rows, width = x_ref.shape
    half = rows // 2
    n_plane = n_dom // 2
    inv_root = 1.0 / width**0.5
    dom = lax.axis_index("dom")
    feat = lax.axis_index("feat")
    core = lax.rem(dom, 2)
    partner = dom + 1 - 2 * core

    def dom_at(step):
        return lax.rem(dom + step + n_dom, n_dom)

    def feat_at(step):
        return lax.rem(feat + step + n_feat, n_feat)

    barrier = pltpu.get_barrier_semaphore()
    for step in range(1, n_dom):
        pl.semaphore_signal(
            barrier, inc=1, device_id=(dom_at(step), feat), device_id_type=MESH
        )
    for step in range(1, n_feat):
        pl.semaphore_signal(
            barrier, inc=1, device_id=(dom, feat_at(step)), device_id_type=MESH
        )

    def send(src, dst, sems, slot, target):
        copy = pltpu.make_async_remote_copy(
            src_ref=src,
            dst_ref=dst,
            send_sem=sems.at[0, slot],
            recv_sem=sems.at[1, slot],
            device_id=target,
            device_id_type=MESH,
        )
        copy.start()
        return copy

    size = size_ref[0]
    lane_ids = lax.broadcasted_iota(jnp.int32, (1, rows), 1)
    row_ids = lax.broadcasted_iota(jnp.int32, (rows, 1), 0)
    alive = jnp.where(row_ids < size, 1.0, 0.0)
    assign_row = assign_ref[...].astype(F32)
    live_row = jnp.where(lane_ids < size, assign_row, -1.0)
    x_own = x_ref[...]
    xp[0] = jnp.concatenate([x_own[:half], x_own[half:]], axis=1)
    am[0] = jnp.broadcast_to(live_row, (8, rows))
    xc[feat] = jnp.concatenate([x_own, cot_ref[...]], axis=1)
    pl.semaphore_wait(barrier, n_dom - 1 + n_feat - 1)

    sent = []
    xp_copies, am_copies = [None], [None]
    for step in range(1, n_dom):
        target = (dom_at(step), feat)
        am_copies.append(send(am.at[0], am.at[step], am_sem, step, target))
        xp_copies.append(send(xp.at[0], xp.at[step], xp_sem, step, target))
    xc_copies = [None]
    for step in range(1, n_feat):
        xc_copies.append(
            send(xc.at[feat], xc.at[feat], xc_sem, step, (dom, feat_at(step)))
        )
    sent += xp_copies[1:] + am_copies[1:] + xc_copies[1:]

    def select(full):
        out = full[:, :width]
        for index in range(1, n_feat):
            out = jnp.where(feat == index, full[:, index * width : (index + 1) * width], out)
        return out

    eye = row_ids == lane_ids
    earlier = lane_ids < row_ids

    def column(row):
        return jnp.sum(jnp.where(eye, row, 0.0), axis=1, keepdims=True)

    assign_col = column(assign_row)
    counts = jnp.zeros((rows, 1), F32)
    before = jnp.zeros((rows, 1), F32)
    sums = jnp.zeros((rows, width), F32)
    for step in range(n_dom):
        if step:
            am_copies[step].wait_recv()
            xp_copies[step].wait_recv()
        same = jnp.where(assign_col == am[step, 0:1, :], 1.0, 0.0)
        block = jnp.sum(same, axis=1, keepdims=True)
        counts = counts + block
        if step:
            before = before + block * jnp.where(step <= dom, 1.0, 0.0)
        else:
            before = jnp.sum(jnp.where(earlier, same, 0.0), axis=1, keepdims=True)
        packed = xp[step]
        piece = jnp.concatenate([packed[:, :width], packed[:, width:]], axis=0)
        sums = sums + dot(same.astype(BF), piece, 1, 0)
    inv_count = counts + 1.0
    cent = (sums / inv_count).astype(BF)
    ct[feat] = jnp.concatenate([cent[:half], cent[half:]], axis=1)
    ct_copies = [None]
    for step in range(1, n_feat):
        ct_copies.append(
            send(ct.at[feat], ct.at[feat], ct_sem, step, (dom, feat_at(step)))
        )
    rep_own = alive * jnp.where(before == 0.0, 1.0, 0.0)
    rep_row = jnp.sum(jnp.where(eye, rep_own, 0.0), axis=0, keepdims=True)
    rep[0] = jnp.broadcast_to(rep_row, (8, rows))
    rep_copies = [None]
    for step in range(1, n_dom):
        rep_copies.append(
            send(rep.at[0], rep.at[step], rep_sem, step, (dom_at(step), feat))
        )
    sent += ct_copies[1:] + rep_copies[1:]

    for step in range(1, n_feat):
        xc_copies[step].wait_recv()
    x_full = jnp.concatenate([xc[index][:, :width] for index in range(n_feat)], axis=1)
    cot_full = jnp.concatenate([xc[index][:, width:] for index in range(n_feat)], axis=1)
    head_rows = pl.ds(pl.multiple_of(feat * width, width), width)
    query = dot(x_full, select(wq_ref[...]), 1, 0).astype(BF)
    g_att = (alive * dot(cot_full, wo_ref[head_rows, :], 1, 1)).astype(BF)
    qg[0] = jnp.concatenate([query, g_att], axis=1)
    qg_copy = send(qg.at[0], qg.at[1], qg_sem, 0, (partner, feat))
    sent.append(qg_copy)

    wkv = jnp.concatenate([select(wk_ref[...]), select(wv_ref[...])], axis=1)
    wo_cols = select(wo_ref[...])
    wq_rows = wq_ref[head_rows, :]
    wk_rows = wk_ref[head_rows, :]
    wv_rows = wv_ref[head_rows, :]

    empty = jnp.full((1, 1), float(CENTROIDS), F32)
    for step in range(n_dom):
        if step:
            rep_copies[step].wait_recv()
        empty = empty - jnp.sum(rep[step, 0:1, :], axis=1, keepdims=True)
    rep_cols = [rep_own] + [column(rep[2 * step, 0:1, :]) for step in range(1, n_plane)]

    for step in range(1, n_feat):
        ct_copies[step].wait_recv()
    cent_full = jnp.concatenate(
        [
            jnp.concatenate([ct[index][:, :width], ct[index][:, width:]], axis=0)
            for index in range(n_feat)
        ],
        axis=1,
    )
    kvb[0] = dot(cent_full, wkv, 1, 0).astype(BF)
    kv_copies = [None]
    for step in range(1, n_plane):
        kv_copies.append(
            send(kvb.at[0], kvb.at[step], kv_sem, step, (dom_at(2 * step), feat))
        )
    sent += kv_copies[1:]

    qg_copy.wait_recv()
    low_lane = lax.broadcasted_iota(jnp.int32, (1, 2 * width), 1) < width
    qg_all = jnp.concatenate([qg[0], qg[1]], axis=0).astype(F32)
    q_low = jnp.where(low_lane, qg_all, 0.0).astype(BF)
    g_high = jnp.where(low_lane, 0.0, qg_all).astype(BF)

    tops, zs, ds = [], [], []
    for step in range(n_plane):
        if step:
            kv_copies[step].wait_recv()
        kv = kvb[step]
        scores = dot(kv, q_low, 1, 1) * inv_root
        g_probs = dot(kv, g_high, 1, 1)
        top = jnp.maximum(jnp.max(scores, axis=0, keepdims=True), 0.0)
        expo = jnp.exp(scores - top)
        e_buf[step] = expo
        g_buf[step] = g_probs
        counted = expo * rep_cols[step]
        tops.append(top)
        zs.append(jnp.sum(counted, axis=0, keepdims=True))
        ds.append(jnp.sum(counted * g_probs, axis=0, keepdims=True))
    top = functools.reduce(jnp.maximum, tops)
    fix = [jnp.exp(one - top) for one in tops]
    z_own = sum(one * scale for one, scale in zip(zs, fix))
    d_own = sum(one * scale for one, scale in zip(ds, fix))
    st[0, 0:1, :] = top
    st[0, 1:2, :] = z_own
    st[0, 2:3, :] = d_own
    st[0, 3:8, :] = jnp.zeros((5, 2 * rows), F32)
    st_copy = send(st.at[0], st.at[1], st_sem, 0, (partner, feat))
    sent.append(st_copy)
    st_copy.wait_recv()
    other = st[1]
    other = jnp.concatenate([other[:, rows:], other[:, :rows]], axis=1)
    top_all = jnp.maximum(top, other[0:1])
    own_fix = jnp.exp(top - top_all)
    other_fix = jnp.exp(other[0:1] - top_all)
    z_all = z_own * own_fix + other[1:2] * other_fix + empty * jnp.exp(-top_all)
    delta = (d_own * own_fix + other[2:3] * other_fix) / z_all

    totals = jnp.zeros((2 * width, 2 * rows), F32)
    gr_copies = [None] * n_plane
    kv_own = None
    for step in list(range(1, n_plane)) + [0]:
        scale = jnp.exp(tops[step] - top_all) / z_all
        probs = e_buf[step] * scale
        probs_low = probs.astype(BF)
        g_scores = (probs * (g_buf[step] - delta) * inv_root).astype(BF)
        partial = dot(g_scores, q_low, 1, 0) + dot(probs_low, g_high, 1, 0)
        if step:
            gsend[step] = partial.astype(BF)
            gr_copies[step] = send(
                gsend.at[step], grecv.at[step], gr_sem, step, (dom_at(-2 * step), feat)
            )
        else:
            kv_own = partial
        kv = kvb[step].astype(F32) * rep_cols[step]
        k_low = jnp.where(low_lane, kv, 0.0).astype(BF)
        v_high = jnp.where(low_lane, 0.0, kv).astype(BF)
        totals = totals + dot(k_low, g_scores, 0, 0) + dot(v_high, probs_low, 0, 0)
    sent += gr_copies[1:]
    aqs[...] = totals[:, rows:]
    ap_copy = send(aqs, aqr, ap_sem, 0, (partner, feat))
    sent.append(ap_copy)
    ap_copy.wait_recv()
    aq[feat] = (totals[:, :rows] + aqr[...]).astype(BF)
    aq_copies = [None]
    for step in range(1, n_feat):
        aq_copies.append(
            send(aq.at[feat], aq.at[feat], aq_sem, step, (dom, feat_at(step)))
        )
    for step in range(1, n_plane):
        gr_copies[step].wait_recv()
        kv_own = kv_own + grecv[step].astype(F32)
    kg[feat] = kv_own.astype(BF)
    kg_copies = [None]
    for step in range(1, n_feat):
        kg_copies.append(
            send(kg.at[feat], kg.at[feat], kg_sem, step, (dom, feat_at(step)))
        )
    sent += aq_copies[1:] + kg_copies[1:]
    for step in range(1, n_feat):
        aq_copies[step].wait_recv()
    gq_full = jnp.concatenate([aq[index][:width] for index in range(n_feat)], axis=0)
    att_full = jnp.concatenate([aq[index][width:] for index in range(n_feat)], axis=0)
    out_ref[...] = (alive * dot(att_full, wo_cols, 0, 0)).astype(BF)
    grad = dot(gq_full, wq_rows, 0, 1)
    for step in range(1, n_feat):
        kg_copies[step].wait_recv()
    cent_grad = jnp.zeros((rows, width), F32)
    for index in range(n_feat):
        spot = slice(index * width, (index + 1) * width)
        stacked = jnp.concatenate([wk_rows[:, spot], wv_rows[:, spot]], axis=1)
        cent_grad = cent_grad + dot(kg[index], stacked, 1, 1)
    gx_ref[...] = (grad + alive * (cent_grad / inv_count)).astype(BF)
    for copy in sent:
        copy.wait_send()


def fused(n_dom, n_feat, node_x, cotangent, assign, part_sizes, w_query, w_key, w_value, w_out):
    rows, width = node_x.shape
    n_plane = n_dom // 2
    vmem = pl.BlockSpec(memory_space=pltpu.VMEM)
    smem = pl.BlockSpec(memory_space=pltpu.SMEM)
    pair = 2 * width

    def sems(count):
        return pltpu.SemaphoreType.DMA((2, count))

    return pl.pallas_call(
        functools.partial(kernel, n_dom, n_feat),
        out_shape=(
            jax.ShapeDtypeStruct((rows, width), BF),
            jax.ShapeDtypeStruct((rows, width), BF),
        ),
        in_specs=[vmem, vmem, vmem, smem, vmem, vmem, vmem, vmem],
        out_specs=(vmem, vmem),
        scratch_shapes=[
            pltpu.VMEM((n_dom, rows // 2, pair), BF),
            pltpu.VMEM((n_dom, 8, rows), F32),
            pltpu.VMEM((n_feat, rows, pair), BF),
            pltpu.VMEM((n_feat, rows // 2, pair), BF),
            pltpu.VMEM((n_dom, 8, rows), F32),
            pltpu.VMEM((n_plane, rows, pair), BF),
            pltpu.VMEM((2, rows, pair), BF),
            pltpu.VMEM((2, 8, 2 * rows), F32),
            pltpu.VMEM((n_plane, rows, pair), BF),
            pltpu.VMEM((n_plane, rows, pair), BF),
            pltpu.VMEM((pair, rows), F32),
            pltpu.VMEM((pair, rows), F32),
            pltpu.VMEM((n_feat, rows, pair), BF),
            pltpu.VMEM((n_feat, pair, rows), BF),
            pltpu.VMEM((n_plane, rows, 2 * rows), F32),
            pltpu.VMEM((n_plane, rows, 2 * rows), F32),
            sems(n_dom),
            sems(n_dom),
            sems(n_feat),
            sems(n_feat),
            sems(n_dom),
            sems(n_plane),
            sems(1),
            sems(1),
            sems(n_plane),
            sems(1),
            sems(n_feat),
            sems(n_feat),
        ],
        compiler_params=pltpu.CompilerParams(collective_id=0, has_side_effects=True),
    )(
        node_x,
        cotangent,
        assign.reshape(1, rows),
        part_sizes,
        w_query,
        w_key,
        w_value,
        w_out,
    )


def trans_dot(left, right):
    return lax.dot_general(
        left, right, (((1,), (1,)), ((), ())), preferred_element_type=jnp.float32
    )


def inner_dot(left, right):
    return lax.dot_general(
        left, right, (((0,), (0,)), ((), ())), preferred_element_type=jnp.float32
    )


def local(node_x, cotangent, assign, part_sizes, w_query, w_key, w_value, w_out):
    row_count, head_width = node_x.shape
    inv_root = 1.0 / head_width**0.5
    offset = lax.axis_index("feat") * head_width
    wq_rows = lax.dynamic_slice_in_dim(w_query, offset, head_width, 0)
    wq_cols = lax.dynamic_slice_in_dim(w_query, offset, head_width, 1)
    wkv_cols = jnp.concatenate(
        [
            lax.dynamic_slice_in_dim(w_key, offset, head_width, 1),
            lax.dynamic_slice_in_dim(w_value, offset, head_width, 1),
        ],
        axis=1,
    )
    wo_rows = lax.dynamic_slice_in_dim(w_out, offset, head_width, 0)
    wo_cols = lax.dynamic_slice_in_dim(w_out, offset, head_width, 1)
    wk_rows = lax.dynamic_slice_in_dim(w_key, offset, head_width, 0).reshape(
        head_width, HEADS, 1, head_width
    )
    wv_rows = lax.dynamic_slice_in_dim(w_value, offset, head_width, 0).reshape(
        head_width, HEADS, 1, head_width
    )
    stacked = jnp.concatenate([wk_rows, wv_rows], axis=2).reshape(
        head_width, HEADS * 2 * head_width
    )
    stacked = jnp.transpose(stacked)
    alive_rows = (jnp.arange(row_count, dtype=jnp.int32) < part_sizes[0]).astype(jnp.float32)[
        :, None
    ]
    x_piece = lax.all_gather(node_x, "feat", axis=1, tiled=True)
    grad_piece = lax.all_gather(cotangent, "feat", axis=1, tiled=True)
    query_sum = jnp.dot(x_piece, wq_cols, preferred_element_type=jnp.float32)
    grad_sum = trans_dot(grad_piece, wo_rows)
    query = query_sum.astype(jnp.bfloat16)
    g_attended = (alive_rows * grad_sum).astype(jnp.bfloat16)
    onehot = (
        (assign[:, None] == jnp.arange(CENTROIDS, dtype=jnp.int32)[None, :]) & (alive_rows > 0.0)
    ).astype(jnp.bfloat16)
    cent_sums = inner_dot(onehot, node_x)
    counts = jnp.sum(onehot.astype(jnp.float32), axis=0)
    owned_sums, owned_counts = (
        lax.psum_scatter(cent_sums, "dom", scatter_dimension=0, tiled=True),
        lax.psum_scatter(counts, "dom", scatter_dimension=0, tiled=True),
    )
    owned_cent = (owned_sums / (owned_counts + 1.0)[:, None]).astype(jnp.bfloat16)
    owned_full = lax.all_gather(owned_cent, "feat", axis=1, tiled=True)
    owned_kv = jnp.dot(owned_full, wkv_cols, preferred_element_type=jnp.float32).astype(
        jnp.bfloat16
    )
    key_value = lax.all_gather(owned_kv, "dom", axis=0, tiled=True)
    keys = key_value[:, :head_width]
    values = key_value[:, head_width:]
    quarter = row_count // 4
    block_ids = jnp.arange(4, dtype=jnp.int32)
    live_blocks = (part_sizes[0] + quarter - 1) // quarter

    def attend_block(query_block, grad_block):
        scores = trans_dot(query_block, keys) * inv_root
        probs = jax.nn.softmax(scores, axis=1)
        probs_low = probs.astype(jnp.bfloat16)
        attended = jnp.dot(probs_low, values, preferred_element_type=jnp.float32).astype(
            jnp.bfloat16
        )
        g_probs = trans_dot(grad_block, values)
        row_delta = jnp.sum(probs * g_probs, axis=1, keepdims=True)
        g_scores = (probs * (g_probs - row_delta) * inv_root).astype(jnp.bfloat16)
        g_query = jnp.dot(g_scores, keys, preferred_element_type=jnp.float32).astype(jnp.bfloat16)
        key_grad = inner_dot(g_scores, query_block)
        value_grad = inner_dot(probs_low, grad_block)
        return (jnp.concatenate([key_grad, value_grad], axis=1), attended, g_query)

    def skip_block(query_block, grad_block):
        return (
            jnp.zeros((CENTROIDS, 2 * head_width), jnp.float32),
            jnp.zeros(query_block.shape, jnp.bfloat16),
            jnp.zeros(query_block.shape, jnp.bfloat16),
        )

    def step_block(running, block_triple):
        query_block, grad_block, active = block_triple
        kv_part, attended, g_query = lax.cond(
            active, attend_block, skip_block, query_block, grad_block
        )
        return (running + kv_part, (attended, g_query))

    start_grads = jnp.zeros((CENTROIDS, 2 * head_width), jnp.float32)
    kv_sum, outputs = lax.scan(
        step_block,
        start_grads,
        (
            query.reshape(4, quarter, head_width),
            g_attended.reshape(4, quarter, head_width),
            block_ids < live_blocks,
        ),
    )
    attended = outputs[0].reshape(row_count, head_width)
    g_query = outputs[1].reshape(row_count, head_width)
    out_wide = jnp.dot(
        lax.all_gather(attended, "feat", axis=1, tiled=True),
        wo_cols,
        preferred_element_type=jnp.float32,
    )
    result_out = (alive_rows * out_wide).astype(jnp.bfloat16)
    owned_grads = lax.psum_scatter(kv_sum, "dom", scatter_dimension=0, tiled=True).astype(
        jnp.bfloat16
    )
    owned_cent_grad = jnp.dot(
        lax.all_gather(owned_grads, "feat", axis=1, tiled=True),
        stacked,
        preferred_element_type=jnp.float32,
    )
    owned_cent_grad = owned_cent_grad / (owned_counts + 1.0)[:, None]
    cent_grad = lax.all_gather(owned_cent_grad, "dom", axis=0, tiled=True)
    from_query = trans_dot(lax.all_gather(g_query, "feat", axis=1, tiled=True), wq_rows)
    grad_x = (from_query + alive_rows * jnp.take(cent_grad, assign, axis=0)).astype(jnp.bfloat16)
    return (result_out, grad_x)


def solution(mesh):
    placed = (P("dom", "feat"), P("dom", "feat"), P("dom"), P("dom"), P(), P(), P(), P())
    n_dom, n_feat = mesh.shape["dom"], mesh.shape["feat"]

    def step(node_x, *rest):
        if n_dom % 2 == 0 and n_dom * node_x.shape[0] < CENTROIDS:
            return fused(n_dom, n_feat, node_x, *rest)
        return local(node_x, *rest)

    return jax.shard_map(
        step,
        mesh=mesh,
        in_specs=placed,
        out_specs=(P("dom", "feat"), P("dom", "feat")),
        check_vma=False,
    )
```

```python
import functools

import jax
import jax.numpy as jnp
from jax import lax
from jax.experimental import pallas as pl
from jax.experimental.pallas import tpu as pltpu
from jax.sharding import PartitionSpec as P

HEADS = 4
CENTROIDS = 4096
MESH = pl.DeviceIdType.MESH
BF = jnp.bfloat16
F32 = jnp.float32


def dot(left, right, left_dim, right_dim):
    return lax.dot_general(
        left, right, (((left_dim,), (right_dim,)), ((), ())), preferred_element_type=F32
    )


def kernel(
    n_dom,
    n_feat,
    x_ref,
    cot_ref,
    assign_ref,
    size_ref,
    wq_ref,
    wk_ref,
    wv_ref,
    wo_ref,
    out_ref,
    gx_ref,
    xp,
    am,
    xc,
    ct,
    rep,
    kvb,
    qg,
    st,
    gsend,
    grecv,
    aqs,
    aqr,
    kg,
    aq,
    e_buf,
    g_buf,
    xp_sem,
    am_sem,
    xc_sem,
    ct_sem,
    rep_sem,
    kv_sem,
    qg_sem,
    st_sem,
    gr_sem,
    ap_sem,
    kg_sem,
    aq_sem,
):
    width, rows = x_ref.shape
    n_plane = n_dom // 2
    inv_root = 1.0 / width**0.5
    dom = lax.axis_index("dom")
    feat = lax.axis_index("feat")
    core = lax.rem(dom, 2)
    partner = dom + 1 - 2 * core

    def dom_at(step):
        return lax.rem(dom + step + n_dom, n_dom)

    def feat_at(step):
        return lax.rem(feat + step + n_feat, n_feat)

    barrier = pltpu.get_barrier_semaphore()
    for step in range(1, n_dom):
        pl.semaphore_signal(
            barrier, inc=1, device_id=(dom_at(step), feat), device_id_type=MESH
        )
    for step in range(1, n_feat):
        pl.semaphore_signal(
            barrier, inc=1, device_id=(dom, feat_at(step)), device_id_type=MESH
        )

    def send(src, dst, sems, slot, target):
        copy = pltpu.make_async_remote_copy(
            src_ref=src,
            dst_ref=dst,
            send_sem=sems.at[0, slot],
            recv_sem=sems.at[1, slot],
            device_id=target,
            device_id_type=MESH,
        )
        copy.start()
        return copy

    size = size_ref[0]
    lane_ids = lax.broadcasted_iota(jnp.int32, (1, rows), 1)
    row_ids = lax.broadcasted_iota(jnp.int32, (rows, 1), 0)
    alive = jnp.where(lane_ids < size, 1.0, 0.0)
    assign_row = assign_ref[...].astype(F32)
    am[0] = jnp.broadcast_to(jnp.where(lane_ids < size, assign_row, -1.0), (8, rows))
    xp[0] = x_ref[...]
    xc[feat, :width] = x_ref[...]
    xc[feat, width:] = cot_ref[...]
    pl.semaphore_wait(barrier, n_dom - 1 + n_feat - 1)

    sent = []
    xp_copies, am_copies = [None], [None]
    for step in range(1, n_dom):
        target = (dom_at(step), feat)
        am_copies.append(send(am.at[0], am.at[step], am_sem, step, target))
        xp_copies.append(send(xp.at[0], xp.at[step], xp_sem, step, target))
    xc_copies = [None]
    for step in range(1, n_feat):
        xc_copies.append(
            send(xc.at[feat], xc.at[feat], xc_sem, step, (dom, feat_at(step)))
        )
    sent += xp_copies[1:] + am_copies[1:] + xc_copies[1:]

    def select(full):
        out = full[:, :width]
        for index in range(1, n_feat):
            out = jnp.where(feat == index, full[:, index * width : (index + 1) * width], out)
        return out

    head_rows = pl.ds(pl.multiple_of(feat * width, width), width)
    wkv = jnp.concatenate([select(wk_ref[...]), select(wv_ref[...])], axis=1)
    wq_cols = select(wq_ref[...])
    wo_cols = select(wo_ref[...])
    wq_rows = wq_ref[head_rows, :]
    wk_rows = wk_ref[head_rows, :]
    wv_rows = wv_ref[head_rows, :]
    wo_rows = wo_ref[head_rows, :]

    eye = row_ids == lane_ids
    earlier = lane_ids < row_ids

    def column(row):
        return jnp.sum(jnp.where(eye, row, 0.0), axis=1, keepdims=True)

    assign_col = column(assign_row)
    mark_ids = lax.broadcasted_iota(jnp.int32, (16, rows), 0)
    sums = jnp.zeros((width + 16, rows), F32)
    before = jnp.zeros((1, rows), F32)
    for step in range(n_dom):
        if step:
            am_copies[step].wait_recv()
        same = jnp.where(assign_col == am[step, 0:1, :], 1.0, 0.0)
        first = jnp.where(step <= dom, 1.0, 0.0) if step else 0.0
        marks = jnp.where(mark_ids == 0, 1.0, jnp.where(mark_ids == 1, first, 0.0))
        if step:
            xp_copies[step].wait_recv()
        else:
            lower = jnp.where(earlier, same, 0.0).astype(BF)
            before = dot(jnp.ones((16, rows), BF), lower, 1, 1)[0:1]
        piece = jnp.concatenate([xp[step], marks.astype(BF)], axis=0)
        sums = sums + dot(piece, same.astype(BF), 1, 1)
    inv_count = sums[width : width + 1] + 1.0
    before = before + sums[width + 1 : width + 2]
    ct[feat] = (sums[:width] / inv_count).astype(BF)
    ct_copies = [None]
    for step in range(1, n_feat):
        ct_copies.append(
            send(ct.at[feat], ct.at[feat], ct_sem, step, (dom, feat_at(step)))
        )
    rep_own = alive * jnp.where(before == 0.0, 1.0, 0.0)
    rep[0] = jnp.broadcast_to(rep_own, (8, rows))
    rep_copies = [None]
    for step in range(1, n_dom):
        rep_copies.append(
            send(rep.at[0], rep.at[step], rep_sem, step, (dom_at(step), feat))
        )
    sent += ct_copies[1:] + rep_copies[1:]

    for step in range(1, n_feat):
        xc_copies[step].wait_recv()
    x_full = jnp.concatenate([xc[index][:width] for index in range(n_feat)], axis=0)
    cot_full = jnp.concatenate([xc[index][width:] for index in range(n_feat)], axis=0)
    qg[0, :width] = dot(wq_cols, x_full, 0, 0).astype(BF)
    qg[0, width:] = (alive * dot(wo_rows, cot_full, 1, 0)).astype(BF)
    qg_copy = send(qg.at[0], qg.at[1], qg_sem, 0, (partner, feat))
    sent.append(qg_copy)

    empty = jnp.full((1, 1), float(CENTROIDS), F32)
    for step in range(n_dom):
        if step:
            rep_copies[step].wait_recv()
        empty = empty - jnp.sum(rep[step, 0:1, :], axis=1, keepdims=True)
    rep_cols = [column(rep[2 * step, 0:1, :]) for step in range(n_plane)]

    qg_copy.wait_recv()
    qg_all = jnp.concatenate([qg[0], qg[1]], axis=1)
    blank = jnp.zeros((width, 2 * rows), BF)
    q_rows = jnp.concatenate([qg_all[:width], blank], axis=0)
    g_rows = jnp.concatenate([blank, qg_all[width:]], axis=0)
    q_low = q_rows.T
    g_high = g_rows.T
    low_lane = lax.broadcasted_iota(jnp.int32, (1, 2 * width), 1) < width

    for step in range(1, n_feat):
        ct_copies[step].wait_recv()
    cent_full = ct[...].reshape(n_feat * width, rows)
    kvb[0] = dot(cent_full, wkv, 0, 0).astype(BF)
    kv_copies = [None]
    for step in range(1, n_plane):
        kv_copies.append(
            send(kvb.at[0], kvb.at[step], kv_sem, step, (dom_at(2 * step), feat))
        )
    sent += kv_copies[1:]

    tops, zs, ds = [], [], []
    for step in range(n_plane):
        if step:
            kv_copies[step].wait_recv()
        kv = kvb[step]
        scores = dot(kv, q_rows, 1, 0) * inv_root
        g_probs = dot(kv, g_rows, 1, 0)
        top = jnp.maximum(jnp.max(scores, axis=0, keepdims=True), 0.0)
        expo = jnp.exp(scores - top)
        e_buf[step] = expo
        g_buf[step] = g_probs
        counted = expo * rep_cols[step]
        tops.append(top)
        zs.append(jnp.sum(counted, axis=0, keepdims=True))
        ds.append(jnp.sum(counted * g_probs, axis=0, keepdims=True))
    top = functools.reduce(jnp.maximum, tops)
    fix = [jnp.exp(one - top) for one in tops]
    z_own = sum(one * scale for one, scale in zip(zs, fix))
    d_own = sum(one * scale for one, scale in zip(ds, fix))
    st[0, 0:1, :] = top
    st[0, 1:2, :] = z_own
    st[0, 2:3, :] = d_own
    st[0, 3:8, :] = jnp.zeros((5, 2 * rows), F32)
    st_copy = send(st.at[0], st.at[1], st_sem, 0, (partner, feat))
    sent.append(st_copy)
    st_copy.wait_recv()
    other = st[1]
    other = jnp.concatenate([other[:, rows:], other[:, :rows]], axis=1)
    top_all = jnp.maximum(top, other[0:1])
    own_fix = jnp.exp(top - top_all)
    other_fix = jnp.exp(other[0:1] - top_all)
    z_all = z_own * own_fix + other[1:2] * other_fix + empty * jnp.exp(-top_all)
    delta = (d_own * own_fix + other[2:3] * other_fix) / z_all

    totals = jnp.zeros((2 * width, 2 * rows), F32)
    gr_copies = [None] * n_plane
    kv_own = None
    for step in list(range(1, n_plane)) + [0]:
        scale = jnp.exp(tops[step] - top_all) / z_all
        probs = e_buf[step] * scale
        probs_low = probs.astype(BF)
        g_scores = (probs * (g_buf[step] - delta) * inv_root).astype(BF)
        partial = dot(g_scores, q_low, 1, 0) + dot(probs_low, g_high, 1, 0)
        if step:
            gsend[step] = partial.astype(BF)
            gr_copies[step] = send(
                gsend.at[step], grecv.at[step], gr_sem, step, (dom_at(-2 * step), feat)
            )
        else:
            kv_own = partial
        kv = kvb[step].astype(F32) * rep_cols[step]
        k_low = jnp.where(low_lane, kv, 0.0).astype(BF)
        v_high = jnp.where(low_lane, 0.0, kv).astype(BF)
        totals = totals + dot(k_low, g_scores, 0, 0) + dot(v_high, probs_low, 0, 0)
    sent += gr_copies[1:]
    aqs[...] = totals[:, rows:]
    ap_copy = send(aqs, aqr, ap_sem, 0, (partner, feat))
    sent.append(ap_copy)
    ap_copy.wait_recv()
    aq[feat] = (totals[:, :rows] + aqr[...]).astype(BF)
    aq_copies = [None]
    for step in range(1, n_feat):
        aq_copies.append(
            send(aq.at[feat], aq.at[feat], aq_sem, step, (dom, feat_at(step)))
        )
    for step in range(1, n_plane):
        gr_copies[step].wait_recv()
        kv_own = kv_own + grecv[step].astype(F32)
    kg[feat] = kv_own.astype(BF)
    kg_copies = [None]
    for step in range(1, n_feat):
        kg_copies.append(
            send(kg.at[feat], kg.at[feat], kg_sem, step, (dom, feat_at(step)))
        )
    sent += aq_copies[1:] + kg_copies[1:]
    for step in range(1, n_feat):
        aq_copies[step].wait_recv()
    gq_full = jnp.concatenate([aq[index][:width] for index in range(n_feat)], axis=0)
    att_full = jnp.concatenate([aq[index][width:] for index in range(n_feat)], axis=0)
    out_ref[...] = (alive * dot(wo_cols, att_full, 0, 0)).astype(BF)
    grad = dot(wq_rows, gq_full, 1, 0)
    for step in range(1, n_feat):
        kg_copies[step].wait_recv()
    cent_grad = jnp.zeros((width, rows), F32)
    for index in range(n_feat):
        spot = slice(index * width, (index + 1) * width)
        stacked = jnp.concatenate([wk_rows[:, spot], wv_rows[:, spot]], axis=1)
        cent_grad = cent_grad + dot(stacked, kg[index], 1, 1)
    gx_ref[...] = (grad + alive * (cent_grad / inv_count)).astype(BF)
    for copy in sent:
        copy.wait_send()


def fused(n_dom, n_feat, node_x, cotangent, assign, part_sizes, w_query, w_key, w_value, w_out):
    rows, width = node_x.shape
    n_plane = n_dom // 2
    vmem = pl.BlockSpec(memory_space=pltpu.VMEM)
    smem = pl.BlockSpec(memory_space=pltpu.SMEM)
    pair = 2 * width

    def sems(count):
        return pltpu.SemaphoreType.DMA((2, count))

    out, grad = pl.pallas_call(
        functools.partial(kernel, n_dom, n_feat),
        out_shape=(
            jax.ShapeDtypeStruct((width, rows), BF),
            jax.ShapeDtypeStruct((width, rows), BF),
        ),
        in_specs=[vmem, vmem, vmem, smem, vmem, vmem, vmem, vmem],
        out_specs=(vmem, vmem),
        scratch_shapes=[
            pltpu.VMEM((n_dom, width, rows), BF),
            pltpu.VMEM((n_dom, 8, rows), F32),
            pltpu.VMEM((n_feat, pair, rows), BF),
            pltpu.VMEM((n_feat, width, rows), BF),
            pltpu.VMEM((n_dom, 8, rows), F32),
            pltpu.VMEM((n_plane, rows, pair), BF),
            pltpu.VMEM((2, pair, rows), BF),
            pltpu.VMEM((2, 8, 2 * rows), F32),
            pltpu.VMEM((n_plane, rows, pair), BF),
            pltpu.VMEM((n_plane, rows, pair), BF),
            pltpu.VMEM((pair, rows), F32),
            pltpu.VMEM((pair, rows), F32),
            pltpu.VMEM((n_feat, rows, pair), BF),
            pltpu.VMEM((n_feat, pair, rows), BF),
            pltpu.VMEM((n_plane, rows, 2 * rows), F32),
            pltpu.VMEM((n_plane, rows, 2 * rows), F32),
            sems(n_dom),
            sems(n_dom),
            sems(n_feat),
            sems(n_feat),
            sems(n_dom),
            sems(n_plane),
            sems(1),
            sems(1),
            sems(n_plane),
            sems(1),
            sems(n_feat),
            sems(n_feat),
        ],
        compiler_params=pltpu.CompilerParams(collective_id=0, has_side_effects=True),
    )(
        node_x.T,
        cotangent.T,
        assign.reshape(1, rows),
        part_sizes,
        w_query,
        w_key,
        w_value,
        w_out,
    )
    return out.T, grad.T


def trans_dot(left, right):
    return lax.dot_general(
        left, right, (((1,), (1,)), ((), ())), preferred_element_type=jnp.float32
    )


def inner_dot(left, right):
    return lax.dot_general(
        left, right, (((0,), (0,)), ((), ())), preferred_element_type=jnp.float32
    )


def local(node_x, cotangent, assign, part_sizes, w_query, w_key, w_value, w_out):
    row_count, head_width = node_x.shape
    inv_root = 1.0 / head_width**0.5
    offset = lax.axis_index("feat") * head_width
    wq_rows = lax.dynamic_slice_in_dim(w_query, offset, head_width, 0)
    wq_cols = lax.dynamic_slice_in_dim(w_query, offset, head_width, 1)
    wkv_cols = jnp.concatenate(
        [
            lax.dynamic_slice_in_dim(w_key, offset, head_width, 1),
            lax.dynamic_slice_in_dim(w_value, offset, head_width, 1),
        ],
        axis=1,
    )
    wo_rows = lax.dynamic_slice_in_dim(w_out, offset, head_width, 0)
    wo_cols = lax.dynamic_slice_in_dim(w_out, offset, head_width, 1)
    wk_rows = lax.dynamic_slice_in_dim(w_key, offset, head_width, 0).reshape(
        head_width, HEADS, 1, head_width
    )
    wv_rows = lax.dynamic_slice_in_dim(w_value, offset, head_width, 0).reshape(
        head_width, HEADS, 1, head_width
    )
    stacked = jnp.concatenate([wk_rows, wv_rows], axis=2).reshape(
        head_width, HEADS * 2 * head_width
    )
    stacked = jnp.transpose(stacked)
    alive_rows = (jnp.arange(row_count, dtype=jnp.int32) < part_sizes[0]).astype(jnp.float32)[
        :, None
    ]
    x_piece = lax.all_gather(node_x, "feat", axis=1, tiled=True)
    grad_piece = lax.all_gather(cotangent, "feat", axis=1, tiled=True)
    query_sum = jnp.dot(x_piece, wq_cols, preferred_element_type=jnp.float32)
    grad_sum = trans_dot(grad_piece, wo_rows)
    query = query_sum.astype(jnp.bfloat16)
    g_attended = (alive_rows * grad_sum).astype(jnp.bfloat16)
    onehot = (
        (assign[:, None] == jnp.arange(CENTROIDS, dtype=jnp.int32)[None, :]) & (alive_rows > 0.0)
    ).astype(jnp.bfloat16)
    cent_sums = inner_dot(onehot, node_x)
    counts = jnp.sum(onehot.astype(jnp.float32), axis=0)
    owned_sums, owned_counts = (
        lax.psum_scatter(cent_sums, "dom", scatter_dimension=0, tiled=True),
        lax.psum_scatter(counts, "dom", scatter_dimension=0, tiled=True),
    )
    owned_cent = (owned_sums / (owned_counts + 1.0)[:, None]).astype(jnp.bfloat16)
    owned_full = lax.all_gather(owned_cent, "feat", axis=1, tiled=True)
    owned_kv = jnp.dot(owned_full, wkv_cols, preferred_element_type=jnp.float32).astype(
        jnp.bfloat16
    )
    key_value = lax.all_gather(owned_kv, "dom", axis=0, tiled=True)
    keys = key_value[:, :head_width]
    values = key_value[:, head_width:]
    quarter = row_count // 4
    block_ids = jnp.arange(4, dtype=jnp.int32)
    live_blocks = (part_sizes[0] + quarter - 1) // quarter

    def attend_block(query_block, grad_block):
        scores = trans_dot(query_block, keys) * inv_root
        probs = jax.nn.softmax(scores, axis=1)
        probs_low = probs.astype(jnp.bfloat16)
        attended = jnp.dot(probs_low, values, preferred_element_type=jnp.float32).astype(
            jnp.bfloat16
        )
        g_probs = trans_dot(grad_block, values)
        row_delta = jnp.sum(probs * g_probs, axis=1, keepdims=True)
        g_scores = (probs * (g_probs - row_delta) * inv_root).astype(jnp.bfloat16)
        g_query = jnp.dot(g_scores, keys, preferred_element_type=jnp.float32).astype(jnp.bfloat16)
        key_grad = inner_dot(g_scores, query_block)
        value_grad = inner_dot(probs_low, grad_block)
        return (jnp.concatenate([key_grad, value_grad], axis=1), attended, g_query)

    def skip_block(query_block, grad_block):
        return (
            jnp.zeros((CENTROIDS, 2 * head_width), jnp.float32),
            jnp.zeros(query_block.shape, jnp.bfloat16),
            jnp.zeros(query_block.shape, jnp.bfloat16),
        )

    def step_block(running, block_triple):
        query_block, grad_block, active = block_triple
        kv_part, attended, g_query = lax.cond(
            active, attend_block, skip_block, query_block, grad_block
        )
        return (running + kv_part, (attended, g_query))

    start_grads = jnp.zeros((CENTROIDS, 2 * head_width), jnp.float32)
    kv_sum, outputs = lax.scan(
        step_block,
        start_grads,
        (
            query.reshape(4, quarter, head_width),
            g_attended.reshape(4, quarter, head_width),
            block_ids < live_blocks,
        ),
    )
    attended = outputs[0].reshape(row_count, head_width)
    g_query = outputs[1].reshape(row_count, head_width)
    out_wide = jnp.dot(
        lax.all_gather(attended, "feat", axis=1, tiled=True),
        wo_cols,
        preferred_element_type=jnp.float32,
    )
    result_out = (alive_rows * out_wide).astype(jnp.bfloat16)
    owned_grads = lax.psum_scatter(kv_sum, "dom", scatter_dimension=0, tiled=True).astype(
        jnp.bfloat16
    )
    owned_cent_grad = jnp.dot(
        lax.all_gather(owned_grads, "feat", axis=1, tiled=True),
        stacked,
        preferred_element_type=jnp.float32,
    )
    owned_cent_grad = owned_cent_grad / (owned_counts + 1.0)[:, None]
    cent_grad = lax.all_gather(owned_cent_grad, "dom", axis=0, tiled=True)
    from_query = trans_dot(lax.all_gather(g_query, "feat", axis=1, tiled=True), wq_rows)
    grad_x = (from_query + alive_rows * jnp.take(cent_grad, assign, axis=0)).astype(jnp.bfloat16)
    return (result_out, grad_x)


def solution(mesh):
    placed = (P("dom", "feat"), P("dom", "feat"), P("dom"), P("dom"), P(), P(), P(), P())
    n_dom, n_feat = mesh.shape["dom"], mesh.shape["feat"]

    def step(node_x, *rest):
        if n_dom % 2 == 0 and n_dom * node_x.shape[0] < CENTROIDS:
            return fused(n_dom, n_feat, node_x, *rest)
        return local(node_x, *rest)

    return jax.shard_map(
        step,
        mesh=mesh,
        in_specs=placed,
        out_specs=(P("dom", "feat"), P("dom", "feat")),
        check_vma=False,
    )
```

```python
import functools

import jax
import jax.numpy as jnp
from jax import lax
from jax.experimental import pallas as pl
from jax.experimental.pallas import tpu as pltpu
from jax.sharding import PartitionSpec as P

HEADS = 4
CENTROIDS = 4096
MESH = pl.DeviceIdType.MESH
BF = jnp.bfloat16
F32 = jnp.float32


def dot(left, right, left_dim, right_dim):
    return lax.dot_general(
        left, right, (((left_dim,), (right_dim,)), ((), ())), preferred_element_type=F32
    )


def kernel(
    n_dom,
    n_feat,
    x_ref,
    cot_ref,
    assign_ref,
    size_ref,
    wq_ref,
    wk_ref,
    wv_ref,
    wo_ref,
    out_ref,
    gx_ref,
    xp,
    am,
    xc,
    ct,
    rep,
    kvb,
    qg,
    st,
    gsend,
    grecv,
    aqs,
    aqr,
    xg,
    aq,
    part,
    gp,
    gpr,
    e_buf,
    g_buf,
    xp_sem,
    am_sem,
    xc_sem,
    ct_sem,
    rep_sem,
    kv_sem,
    qg_sem,
    st_sem,
    gr_sem,
    ap_sem,
    gp_sem,
    aq_sem,
    co_sem,
):
    width, rows = x_ref.shape
    n_plane = n_dom // 2
    inv_root = 1.0 / width**0.5
    dom = lax.axis_index("dom")
    feat = lax.axis_index("feat")
    core = lax.rem(dom, 2)
    partner = dom + 1 - 2 * core

    def dom_at(step):
        return lax.rem(dom + step + n_dom, n_dom)

    def feat_at(step):
        return lax.rem(feat + step + n_feat, n_feat)

    barrier = pltpu.get_barrier_semaphore()
    for step in range(1, n_dom):
        pl.semaphore_signal(
            barrier, inc=1, device_id=(dom_at(step), feat), device_id_type=MESH
        )
    for step in range(1, n_feat):
        pl.semaphore_signal(
            barrier, inc=1, device_id=(dom, feat_at(step)), device_id_type=MESH
        )

    def send(src, dst, sems, slot, target):
        copy = pltpu.make_async_remote_copy(
            src_ref=src,
            dst_ref=dst,
            send_sem=sems.at[0, slot],
            recv_sem=sems.at[1, slot],
            device_id=target,
            device_id_type=MESH,
        )
        copy.start()
        return copy

    size = size_ref[0]
    lane_ids = lax.broadcasted_iota(jnp.int32, (1, rows), 1)
    row_ids = lax.broadcasted_iota(jnp.int32, (rows, 1), 0)
    alive = jnp.where(lane_ids < size, 1.0, 0.0)
    assign_row = assign_ref[...].astype(F32)
    am[0] = jnp.broadcast_to(jnp.where(lane_ids < size, assign_row, -1.0), (8, rows))
    xp[0] = x_ref[...]
    xg[feat] = x_ref[...]
    xc[feat] = cot_ref[...]

    def select(full):
        out = full[:, :width]
        for index in range(1, n_feat):
            out = jnp.where(feat == index, full[:, index * width : (index + 1) * width], out)
        return out

    head_rows = pl.ds(pl.multiple_of(feat * width, width), width)
    wkv = jnp.concatenate([select(wk_ref[...]), select(wv_ref[...])], axis=1)
    wq_cols = select(wq_ref[...])
    wo_cols = select(wo_ref[...])
    wo_rows = wo_ref[head_rows, :]

    eye = row_ids == lane_ids
    earlier = lane_ids < row_ids

    def column(row):
        return jnp.sum(jnp.where(eye, row, 0.0), axis=1, keepdims=True)

    assign_col = column(assign_row)
    mark_ids = lax.broadcasted_iota(jnp.int32, (16, rows), 0)

    def add_block(step, sums):
        same = jnp.where(assign_col == am[step, 0:1, :], 1.0, 0.0)
        first = jnp.where(step <= dom, 1.0, 0.0) if step else 0.0
        marks = jnp.where(mark_ids == 0, 1.0, jnp.where(mark_ids == 1, first, 0.0))
        piece = jnp.concatenate([xp[step], marks.astype(BF)], axis=0)
        return sums + dot(piece, same.astype(BF), 1, 1)

    own_live = jnp.where(lane_ids < size, assign_row, -1.0)
    lower = jnp.where(earlier & (assign_col == own_live), 1.0, 0.0).astype(BF)
    before = dot(jnp.ones((16, rows), BF), lower, 1, 1)[0:1]
    sums = add_block(0, jnp.zeros((width + 16, rows), F32))

    pl.semaphore_wait(barrier, n_dom - 1 + n_feat - 1)
    sent = []
    xp_copies, am_copies, xg_copies = [None], [None], [None]
    for step in range(1, n_dom):
        target = (dom_at(step), feat)
        am_copies.append(send(am.at[0], am.at[step], am_sem, step, target))
        xp_copies.append(send(xp.at[0], xp.at[step], xp_sem, step, target))
    for step in range(1, n_feat):
        xg_copies.append(
            send(xg.at[feat], xg.at[feat], xc_sem, step, (dom, feat_at(step)))
        )
    sent += xp_copies[1:] + am_copies[1:] + xg_copies[1:]
    for step in range(1, n_dom):
        am_copies[step].wait_recv()
        xp_copies[step].wait_recv()
        sums = add_block(step, sums)
    inv_count = sums[width : width + 1] + 1.0
    before = before + sums[width + 1 : width + 2]
    ct[feat] = (sums[:width] / inv_count).astype(BF)
    ct_copies = [None]
    for step in range(1, n_feat):
        ct_copies.append(
            send(ct.at[feat], ct.at[feat], ct_sem, step, (dom, feat_at(step)))
        )
    xc_copies = [None]
    for step in range(1, n_feat):
        xc_copies.append(
            send(xc.at[feat], xc.at[feat], co_sem, step, (dom, feat_at(step)))
        )
    rep_own = alive * jnp.where(before == 0.0, 1.0, 0.0)
    rep[0] = jnp.broadcast_to(rep_own, (8, rows))
    rep_copies = [None]
    for step in range(1, n_dom):
        rep_copies.append(
            send(rep.at[0], rep.at[step], rep_sem, step, (dom_at(step), feat))
        )
    sent += ct_copies[1:] + rep_copies[1:] + xc_copies[1:]

    for step in range(1, n_feat):
        xg_copies[step].wait_recv()
    qg[0, :width] = dot(wq_cols, xg[...].reshape(n_feat * width, rows), 0, 0).astype(BF)

    empty = jnp.full((1, 1), float(CENTROIDS), F32)
    for step in range(n_dom):
        if step:
            rep_copies[step].wait_recv()
        empty = empty - jnp.sum(rep[step, 0:1, :], axis=1, keepdims=True)
    rep_cols = [column(rep[2 * step, 0:1, :]) for step in range(n_plane)]

    for step in range(1, n_feat):
        ct_copies[step].wait_recv()
    cent_full = ct[...].reshape(n_feat * width, rows)
    kvb[0] = dot(cent_full, wkv, 0, 0).astype(BF)
    kv_copies = [None]
    for step in range(1, n_plane):
        kv_copies.append(
            send(kvb.at[0], kvb.at[step], kv_sem, step, (dom_at(2 * step), feat))
        )
    sent += kv_copies[1:]

    for step in range(1, n_feat):
        xc_copies[step].wait_recv()
    cot_full = xc[...].reshape(n_feat * width, rows)
    qg[0, width:] = (alive * dot(wo_rows, cot_full, 1, 0)).astype(BF)
    qg_copy = send(qg.at[0], qg.at[1], qg_sem, 0, (partner, feat))
    sent.append(qg_copy)
    qg_copy.wait_recv()
    qg_all = jnp.concatenate([qg[0], qg[1]], axis=1)
    blank = jnp.zeros((width, 2 * rows), BF)
    q_rows = jnp.concatenate([qg_all[:width], blank], axis=0)
    g_rows = jnp.concatenate([blank, qg_all[width:]], axis=0)
    q_low = q_rows.T
    g_high = g_rows.T
    low_lane = lax.broadcasted_iota(jnp.int32, (1, 2 * width), 1) < width

    tops, zs, ds = [], [], []
    for step in range(n_plane):
        if step:
            kv_copies[step].wait_recv()
        kv = kvb[step]
        scores = dot(kv, q_rows, 1, 0) * inv_root
        g_probs = dot(kv, g_rows, 1, 0)
        top = jnp.maximum(jnp.max(scores, axis=0, keepdims=True), 0.0)
        expo = jnp.exp(scores - top)
        e_buf[step] = expo
        g_buf[step] = g_probs
        counted = expo * rep_cols[step]
        tops.append(top)
        zs.append(jnp.sum(counted, axis=0, keepdims=True))
        ds.append(jnp.sum(counted * g_probs, axis=0, keepdims=True))
    top = functools.reduce(jnp.maximum, tops)
    fix = [jnp.exp(one - top) for one in tops]
    z_own = sum(one * scale for one, scale in zip(zs, fix))
    d_own = sum(one * scale for one, scale in zip(ds, fix))
    st[0, 0:1, :] = top
    st[0, 1:2, :] = z_own
    st[0, 2:3, :] = d_own
    st[0, 3:8, :] = jnp.zeros((5, 2 * rows), F32)
    st_copy = send(st.at[0], st.at[1], st_sem, 0, (partner, feat))
    sent.append(st_copy)
    st_copy.wait_recv()
    other = st[1]
    other = jnp.concatenate([other[:, rows:], other[:, :rows]], axis=1)
    top_all = jnp.maximum(top, other[0:1])
    own_fix = jnp.exp(top - top_all)
    other_fix = jnp.exp(other[0:1] - top_all)
    z_all = z_own * own_fix + other[1:2] * other_fix + empty * jnp.exp(-top_all)
    delta = (d_own * own_fix + other[2:3] * other_fix) / z_all

    totals = jnp.zeros((2 * width, 2 * rows), F32)
    gr_copies = [None] * n_plane
    kv_own = None
    for step in list(range(1, n_plane)) + [0]:
        scale = jnp.exp(tops[step] - top_all) / z_all
        probs = e_buf[step] * scale
        probs_low = probs.astype(BF)
        g_scores = (probs * (g_buf[step] - delta) * inv_root).astype(BF)
        partial = dot(g_scores, q_low, 1, 0) + dot(probs_low, g_high, 1, 0)
        if step:
            gsend[step] = partial.astype(BF)
            gr_copies[step] = send(
                gsend.at[step], grecv.at[step], gr_sem, step, (dom_at(-2 * step), feat)
            )
        else:
            kv_own = partial
        kv = kvb[step].astype(F32) * rep_cols[step]
        k_low = jnp.where(low_lane, kv, 0.0).astype(BF)
        v_high = jnp.where(low_lane, 0.0, kv).astype(BF)
        totals = totals + dot(k_low, g_scores, 0, 0) + dot(v_high, probs_low, 0, 0)
    sent += gr_copies[1:]
    aqs[...] = totals[:, rows:]
    ap_copy = send(aqs, aqr, ap_sem, 0, (partner, feat))
    sent.append(ap_copy)
    ap_copy.wait_recv()
    whole = (totals[:, :rows] + aqr[...]).astype(BF)
    aq[feat] = whole[width:]
    aq_copies = [None]
    for step in range(1, n_feat):
        aq_copies.append(
            send(aq.at[feat], aq.at[feat], aq_sem, step, (dom, feat_at(step)))
        )
    grad = dot(wq_cols, whole[:width], 1, 0)
    for step in range(1, n_plane):
        gr_copies[step].wait_recv()
        kv_own = kv_own + grecv[step].astype(F32)
    grad = grad + (alive / inv_count) * dot(wkv, kv_own.astype(BF), 1, 1)
    grad = grad.reshape(n_feat, width, rows)
    part[...] = grad
    gp[...] = grad.astype(BF)
    gp_copies = [None]
    for step in range(1, n_feat):
        target = feat_at(step)
        gp_copies.append(send(gp.at[target], gpr.at[step], gp_sem, step, (dom, target)))
    sent += aq_copies[1:] + gp_copies[1:]
    for step in range(1, n_feat):
        aq_copies[step].wait_recv()
    att_full = aq[...].reshape(n_feat * width, rows)
    out_ref[...] = (alive * dot(wo_cols, att_full, 0, 0)).astype(BF)
    total = part[feat]
    for step in range(1, n_feat):
        gp_copies[step].wait_recv()
        total = total + gpr[step].astype(F32)
    gx_ref[...] = total.astype(BF)
    for copy in sent:
        copy.wait_send()


def fused(n_dom, n_feat, node_x, cotangent, assign, part_sizes, w_query, w_key, w_value, w_out):
    rows, width = node_x.shape
    n_plane = n_dom // 2
    vmem = pl.BlockSpec(memory_space=pltpu.VMEM)
    smem = pl.BlockSpec(memory_space=pltpu.SMEM)
    pair = 2 * width

    def sems(count):
        return pltpu.SemaphoreType.DMA((2, count))

    out, grad = pl.pallas_call(
        functools.partial(kernel, n_dom, n_feat),
        out_shape=(
            jax.ShapeDtypeStruct((width, rows), BF),
            jax.ShapeDtypeStruct((width, rows), BF),
        ),
        in_specs=[vmem, vmem, vmem, smem, vmem, vmem, vmem, vmem],
        out_specs=(vmem, vmem),
        scratch_shapes=[
            pltpu.VMEM((n_dom, width, rows), BF),
            pltpu.VMEM((n_dom, 8, rows), F32),
            pltpu.VMEM((n_feat, width, rows), BF),
            pltpu.VMEM((n_feat, width, rows), BF),
            pltpu.VMEM((n_dom, 8, rows), F32),
            pltpu.VMEM((n_plane, rows, pair), BF),
            pltpu.VMEM((2, pair, rows), BF),
            pltpu.VMEM((2, 8, 2 * rows), F32),
            pltpu.VMEM((n_plane, rows, pair), BF),
            pltpu.VMEM((n_plane, rows, pair), BF),
            pltpu.VMEM((pair, rows), F32),
            pltpu.VMEM((pair, rows), F32),
            pltpu.VMEM((n_feat, width, rows), BF),
            pltpu.VMEM((n_feat, width, rows), BF),
            pltpu.VMEM((n_feat, width, rows), F32),
            pltpu.VMEM((n_feat, width, rows), BF),
            pltpu.VMEM((n_feat, width, rows), BF),
            pltpu.VMEM((n_plane, rows, 2 * rows), F32),
            pltpu.VMEM((n_plane, rows, 2 * rows), F32),
            sems(n_dom),
            sems(n_dom),
            sems(n_feat),
            sems(n_feat),
            sems(n_dom),
            sems(n_plane),
            sems(1),
            sems(1),
            sems(n_plane),
            sems(1),
            sems(n_feat),
            sems(n_feat),
            sems(n_feat),
        ],
        compiler_params=pltpu.CompilerParams(collective_id=0, has_side_effects=True),
    )(
        node_x.T,
        cotangent.T,
        assign.reshape(1, rows),
        part_sizes,
        w_query,
        w_key,
        w_value,
        w_out,
    )
    return out.T, grad.T


def trans_dot(left, right):
    return lax.dot_general(
        left, right, (((1,), (1,)), ((), ())), preferred_element_type=jnp.float32
    )


def inner_dot(left, right):
    return lax.dot_general(
        left, right, (((0,), (0,)), ((), ())), preferred_element_type=jnp.float32
    )


def local(node_x, cotangent, assign, part_sizes, w_query, w_key, w_value, w_out):
    row_count, head_width = node_x.shape
    inv_root = 1.0 / head_width**0.5
    offset = lax.axis_index("feat") * head_width
    wq_rows = lax.dynamic_slice_in_dim(w_query, offset, head_width, 0)
    wq_cols = lax.dynamic_slice_in_dim(w_query, offset, head_width, 1)
    wkv_cols = jnp.concatenate(
        [
            lax.dynamic_slice_in_dim(w_key, offset, head_width, 1),
            lax.dynamic_slice_in_dim(w_value, offset, head_width, 1),
        ],
        axis=1,
    )
    wo_rows = lax.dynamic_slice_in_dim(w_out, offset, head_width, 0)
    wo_cols = lax.dynamic_slice_in_dim(w_out, offset, head_width, 1)
    wk_rows = lax.dynamic_slice_in_dim(w_key, offset, head_width, 0).reshape(
        head_width, HEADS, 1, head_width
    )
    wv_rows = lax.dynamic_slice_in_dim(w_value, offset, head_width, 0).reshape(
        head_width, HEADS, 1, head_width
    )
    stacked = jnp.concatenate([wk_rows, wv_rows], axis=2).reshape(
        head_width, HEADS * 2 * head_width
    )
    stacked = jnp.transpose(stacked)
    alive_rows = (jnp.arange(row_count, dtype=jnp.int32) < part_sizes[0]).astype(jnp.float32)[
        :, None
    ]
    x_piece = lax.all_gather(node_x, "feat", axis=1, tiled=True)
    grad_piece = lax.all_gather(cotangent, "feat", axis=1, tiled=True)
    query_sum = jnp.dot(x_piece, wq_cols, preferred_element_type=jnp.float32)
    grad_sum = trans_dot(grad_piece, wo_rows)
    query = query_sum.astype(jnp.bfloat16)
    g_attended = (alive_rows * grad_sum).astype(jnp.bfloat16)
    onehot = (
        (assign[:, None] == jnp.arange(CENTROIDS, dtype=jnp.int32)[None, :]) & (alive_rows > 0.0)
    ).astype(jnp.bfloat16)
    cent_sums = inner_dot(onehot, node_x)
    counts = jnp.sum(onehot.astype(jnp.float32), axis=0)
    owned_sums, owned_counts = (
        lax.psum_scatter(cent_sums, "dom", scatter_dimension=0, tiled=True),
        lax.psum_scatter(counts, "dom", scatter_dimension=0, tiled=True),
    )
    owned_cent = (owned_sums / (owned_counts + 1.0)[:, None]).astype(jnp.bfloat16)
    owned_full = lax.all_gather(owned_cent, "feat", axis=1, tiled=True)
    owned_kv = jnp.dot(owned_full, wkv_cols, preferred_element_type=jnp.float32).astype(
        jnp.bfloat16
    )
    key_value = lax.all_gather(owned_kv, "dom", axis=0, tiled=True)
    keys = key_value[:, :head_width]
    values = key_value[:, head_width:]
    quarter = row_count // 4
    block_ids = jnp.arange(4, dtype=jnp.int32)
    live_blocks = (part_sizes[0] + quarter - 1) // quarter

    def attend_block(query_block, grad_block):
        scores = trans_dot(query_block, keys) * inv_root
        probs = jax.nn.softmax(scores, axis=1)
        probs_low = probs.astype(jnp.bfloat16)
        attended = jnp.dot(probs_low, values, preferred_element_type=jnp.float32).astype(
            jnp.bfloat16
        )
        g_probs = trans_dot(grad_block, values)
        row_delta = jnp.sum(probs * g_probs, axis=1, keepdims=True)
        g_scores = (probs * (g_probs - row_delta) * inv_root).astype(jnp.bfloat16)
        g_query = jnp.dot(g_scores, keys, preferred_element_type=jnp.float32).astype(jnp.bfloat16)
        key_grad = inner_dot(g_scores, query_block)
        value_grad = inner_dot(probs_low, grad_block)
        return (jnp.concatenate([key_grad, value_grad], axis=1), attended, g_query)

    def skip_block(query_block, grad_block):
        return (
            jnp.zeros((CENTROIDS, 2 * head_width), jnp.float32),
            jnp.zeros(query_block.shape, jnp.bfloat16),
            jnp.zeros(query_block.shape, jnp.bfloat16),
        )

    def step_block(running, block_triple):
        query_block, grad_block, active = block_triple
        kv_part, attended, g_query = lax.cond(
            active, attend_block, skip_block, query_block, grad_block
        )
        return (running + kv_part, (attended, g_query))

    start_grads = jnp.zeros((CENTROIDS, 2 * head_width), jnp.float32)
    kv_sum, outputs = lax.scan(
        step_block,
        start_grads,
        (
            query.reshape(4, quarter, head_width),
            g_attended.reshape(4, quarter, head_width),
            block_ids < live_blocks,
        ),
    )
    attended = outputs[0].reshape(row_count, head_width)
    g_query = outputs[1].reshape(row_count, head_width)
    out_wide = jnp.dot(
        lax.all_gather(attended, "feat", axis=1, tiled=True),
        wo_cols,
        preferred_element_type=jnp.float32,
    )
    result_out = (alive_rows * out_wide).astype(jnp.bfloat16)
    owned_grads = lax.psum_scatter(kv_sum, "dom", scatter_dimension=0, tiled=True).astype(
        jnp.bfloat16
    )
    owned_cent_grad = jnp.dot(
        lax.all_gather(owned_grads, "feat", axis=1, tiled=True),
        stacked,
        preferred_element_type=jnp.float32,
    )
    owned_cent_grad = owned_cent_grad / (owned_counts + 1.0)[:, None]
    cent_grad = lax.all_gather(owned_cent_grad, "dom", axis=0, tiled=True)
    from_query = trans_dot(lax.all_gather(g_query, "feat", axis=1, tiled=True), wq_rows)
    grad_x = (from_query + alive_rows * jnp.take(cent_grad, assign, axis=0)).astype(jnp.bfloat16)
    return (result_out, grad_x)


def solution(mesh):
    placed = (P("dom", "feat"), P("dom", "feat"), P("dom"), P("dom"), P(), P(), P(), P())
    n_dom, n_feat = mesh.shape["dom"], mesh.shape["feat"]

    def step(node_x, *rest):
        if n_dom % 2 == 0 and n_dom * node_x.shape[0] < CENTROIDS:
            return fused(n_dom, n_feat, node_x, *rest)
        return local(node_x, *rest)

    return jax.shard_map(
        step,
        mesh=mesh,
        in_specs=placed,
        out_specs=(P("dom", "feat"), P("dom", "feat")),
        check_vma=False,
    )
```

```python
import functools

import jax
import jax.numpy as jnp
from jax import lax
from jax.experimental import pallas as pl
from jax.experimental.pallas import tpu as pltpu
from jax.sharding import PartitionSpec as P

HEADS = 4
CENTROIDS = 4096
MESH = pl.DeviceIdType.MESH
BF = jnp.bfloat16
F32 = jnp.float32


def dot(left, right, left_dim, right_dim):
    return lax.dot_general(
        left, right, (((left_dim,), (right_dim,)), ((), ())), preferred_element_type=F32
    )


def kernel(
    n_dom,
    n_feat,
    x_ref,
    cot_ref,
    assign_ref,
    size_ref,
    wq_ref,
    wk_ref,
    wv_ref,
    wo_ref,
    out_ref,
    xp,
    am,
    xc,
    ct,
    rep,
    kvb,
    qg,
    st,
    gsend,
    grecv,
    aqs,
    aqr,
    xg,
    aq,
    part,
    gp,
    gpr,
    e_buf,
    g_buf,
    masked,
    low_buf,
    xp_sem,
    am_sem,
    xc_sem,
    ct_sem,
    rep_sem,
    kv_sem,
    qg_sem,
    st_sem,
    gr_sem,
    ap_sem,
    gp_sem,
    aq_sem,
    co_sem,
):
    width, rows = x_ref.shape
    n_plane = n_dom // 2
    inv_root = 1.0 / width**0.5
    dom = lax.axis_index("dom")
    feat = lax.axis_index("feat")
    core = lax.rem(dom, 2)
    partner = dom + 1 - 2 * core

    def dom_at(step):
        return lax.rem(dom + step + n_dom, n_dom)

    def source(step):
        if n_plane == 4:
            plane = dom // 2
            across, along = plane // 2, lax.rem(plane, 2)
            if step != 3:
                across = 1 - across
            if step != 2:
                along = 1 - along
            return 4 * across + 2 * along + core
        return dom_at(-2 * step)

    def reader(step):
        return source(step) if n_plane == 4 else dom_at(2 * step)

    def feat_at(step):
        return lax.rem(feat + step + n_feat, n_feat)

    barrier = pltpu.get_barrier_semaphore()
    for step in range(1, n_dom):
        pl.semaphore_signal(
            barrier, inc=1, device_id=(dom_at(step), feat), device_id_type=MESH
        )
    for step in range(1, n_feat):
        pl.semaphore_signal(
            barrier, inc=1, device_id=(dom, feat_at(step)), device_id_type=MESH
        )

    def send(src, dst, sems, slot, target):
        copy = pltpu.make_async_remote_copy(
            src_ref=src,
            dst_ref=dst,
            send_sem=sems.at[0, slot],
            recv_sem=sems.at[1, slot],
            device_id=target,
            device_id_type=MESH,
        )
        copy.start()
        return copy

    size = size_ref[0]
    lane_ids = lax.broadcasted_iota(jnp.int32, (1, rows), 1)
    row_ids = lax.broadcasted_iota(jnp.int32, (rows, 1), 0)
    alive = jnp.where(lane_ids < size, 1.0, 0.0)
    assign_row = assign_ref[...].astype(F32)
    am[0] = jnp.broadcast_to(jnp.where(lane_ids < size, assign_row, -1.0), (8, rows))
    xp[0] = x_ref[...]
    xg[feat] = x_ref[...]
    xc[feat] = cot_ref[...]

    def select(full):
        out = full[:, :width]
        for index in range(1, n_feat):
            out = jnp.where(feat == index, full[:, index * width : (index + 1) * width], out)
        return out

    head_rows = pl.ds(pl.multiple_of(feat * width, width), width)
    wkv = jnp.concatenate([select(wk_ref[...]), select(wv_ref[...])], axis=1)
    wq_cols = select(wq_ref[...])
    wo_cols = select(wo_ref[...])
    wo_rows = wo_ref[head_rows, :]

    eye = row_ids == lane_ids
    earlier = lane_ids < row_ids

    def column(row):
        return jnp.sum(jnp.where(eye, row, 0.0), axis=1, keepdims=True)

    assign_col = column(assign_row)
    mark_ids = lax.broadcasted_iota(jnp.int32, (16, rows), 0)

    def add_block(step, sums):
        same = jnp.where(assign_col == am[step, 0:1, :], 1.0, 0.0)
        first = jnp.where(step <= dom, 1.0, 0.0) if step else 0.0
        marks = jnp.where(mark_ids == 0, 1.0, jnp.where(mark_ids == 1, first, 0.0))
        piece = jnp.concatenate([xp[step], marks.astype(BF)], axis=0)
        return sums + dot(piece, same.astype(BF), 1, 1)

    own_live = jnp.where(lane_ids < size, assign_row, -1.0)
    lower = jnp.where(earlier & (assign_col == own_live), 1.0, 0.0).astype(BF)
    before = dot(jnp.ones((16, rows), BF), lower, 1, 1)[0:1]
    sums = add_block(0, jnp.zeros((width + 16, rows), F32))

    pl.semaphore_wait(barrier, n_dom - 1 + n_feat - 1)
    sent = []
    xp_copies, am_copies, xg_copies = [None], [None], [None]
    for step in range(1, n_dom):
        target = (dom_at(step), feat)
        am_copies.append(send(am.at[0], am.at[step], am_sem, step, target))
        xp_copies.append(send(xp.at[0], xp.at[step], xp_sem, step, target))
    for step in range(1, n_feat):
        xg_copies.append(
            send(xg.at[feat], xg.at[feat], xc_sem, step, (dom, feat_at(step)))
        )
    sent += xp_copies[1:] + am_copies[1:] + xg_copies[1:]
    for step in range(1, n_dom):
        am_copies[step].wait_recv()
        xp_copies[step].wait_recv()
        sums = add_block(step, sums)
    inv_count = sums[width : width + 1] + 1.0
    before = before + sums[width + 1 : width + 2]
    ct[feat] = (sums[:width] / inv_count).astype(BF)
    ct_copies = [None]
    for step in range(1, n_feat):
        ct_copies.append(
            send(ct.at[feat], ct.at[feat], ct_sem, step, (dom, feat_at(step)))
        )
    xc_copies = [None]
    for step in range(1, n_feat):
        xc_copies.append(
            send(xc.at[feat], xc.at[feat], co_sem, step, (dom, feat_at(step)))
        )
    rep_own = alive * jnp.where(before == 0.0, 1.0, 0.0)
    rep[0] = jnp.broadcast_to(rep_own, (8, rows))
    rep_copies = [None]
    for step in range(1, n_dom):
        rep_copies.append(
            send(rep.at[0], rep.at[step], rep_sem, step, (dom_at(step), feat))
        )
    sent += ct_copies[1:] + rep_copies[1:] + xc_copies[1:]

    for step in range(1, n_feat):
        xg_copies[step].wait_recv()
    qg[0, :width] = dot(wq_cols, xg[...].reshape(n_feat * width, rows), 0, 0).astype(BF)

    empty = jnp.full((1, 1), float(CENTROIDS), F32)
    for step in range(n_dom):
        if step:
            rep_copies[step].wait_recv()
        empty = empty - jnp.sum(rep[step, 0:1, :], axis=1, keepdims=True)
    rep_cols = [column(rep[0, 0:1, :])]
    for step in range(1, n_plane):
        slot = lax.rem(dom - source(step) + n_dom, n_dom)
        rep_cols.append(column(rep[slot, 0:1, :]))

    for step in range(1, n_feat):
        ct_copies[step].wait_recv()
    cent_full = ct[...].reshape(n_feat * width, rows)
    kvb[0] = dot(cent_full, wkv, 0, 0).astype(BF)
    kv_copies = [None]
    for step in range(1, n_plane):
        kv_copies.append(
            send(kvb.at[0], kvb.at[step], kv_sem, step, (reader(step), feat))
        )
    sent += kv_copies[1:]

    for step in range(1, n_feat):
        xc_copies[step].wait_recv()
    cot_full = xc[...].reshape(n_feat * width, rows)
    qg[0, width:] = (alive * dot(wo_rows, cot_full, 1, 0)).astype(BF)
    qg_copy = send(qg.at[0], qg.at[1], qg_sem, 0, (partner, feat))
    sent.append(qg_copy)
    qg_copy.wait_recv()
    qg_all = jnp.concatenate([qg[0], qg[1]], axis=1)
    blank = jnp.zeros((width, 2 * rows), BF)
    q_rows = jnp.concatenate([qg_all[:width], blank], axis=0)
    g_rows = jnp.concatenate([blank, qg_all[width:]], axis=0)
    q_low = q_rows.T
    g_high = g_rows.T
    low_lane = lax.broadcasted_iota(jnp.int32, (1, 2 * width), 1) < width

    tops, zs, ds = [], [], []
    for step in range(n_plane):
        if step:
            kv_copies[step].wait_recv()
        kv = kvb[step]
        scores = dot(kv, q_rows, 1, 0) * inv_root
        g_probs = dot(kv, g_rows, 1, 0)
        top = jnp.maximum(jnp.max(scores, axis=0, keepdims=True), 0.0)
        expo = jnp.exp(scores - top)
        e_buf[step] = expo
        g_buf[step] = g_probs
        counted = expo * rep_cols[step]
        tops.append(top)
        zs.append(jnp.sum(counted, axis=0, keepdims=True))
        ds.append(jnp.sum(counted * g_probs, axis=0, keepdims=True))
    top = functools.reduce(jnp.maximum, tops)
    fix = [jnp.exp(one - top) for one in tops]
    z_own = sum(one * scale for one, scale in zip(zs, fix))
    d_own = sum(one * scale for one, scale in zip(ds, fix))
    st[0, 0:1, :] = top
    st[0, 1:2, :] = z_own
    st[0, 2:3, :] = d_own
    st[0, 3:8, :] = jnp.zeros((5, 2 * rows), F32)
    st_copy = send(st.at[0], st.at[1], st_sem, 0, (partner, feat))
    sent.append(st_copy)
    for step in range(n_plane):
        kv = kvb[step].astype(F32) * rep_cols[step]
        masked[0, :, step * rows : (step + 1) * rows] = jnp.where(low_lane, kv, 0.0).astype(BF).T
        masked[1, :, step * rows : (step + 1) * rows] = jnp.where(low_lane, 0.0, kv).astype(BF).T
    st_copy.wait_recv()
    other = st[1]
    other = jnp.concatenate([other[:, rows:], other[:, :rows]], axis=1)
    top_all = jnp.maximum(top, other[0:1])
    own_fix = jnp.exp(top - top_all)
    other_fix = jnp.exp(other[0:1] - top_all)
    z_all = z_own * own_fix + other[1:2] * other_fix + empty * jnp.exp(-top_all)
    delta = (d_own * own_fix + other[2:3] * other_fix) / z_all

    gr_copies = [None] * n_plane
    kv_own = None
    for step in list(range(1, n_plane)) + [0]:
        scale = jnp.exp(tops[step] - top_all) / z_all
        probs = e_buf[step] * scale
        probs_low = probs.astype(BF)
        g_scores = (probs * (g_buf[step] - delta) * inv_root).astype(BF)
        low_buf[0, step * rows : (step + 1) * rows, :] = g_scores
        low_buf[1, step * rows : (step + 1) * rows, :] = probs_low
        partial = dot(g_scores, q_low, 1, 0) + dot(probs_low, g_high, 1, 0)
        if step:
            gsend[step] = partial.astype(BF)
            gr_copies[step] = send(
                gsend.at[step], grecv.at[step], gr_sem, step, (source(step), feat)
            )
        else:
            kv_own = partial
    totals = dot(masked[0], low_buf[0], 1, 0) + dot(masked[1], low_buf[1], 1, 0)
    sent += gr_copies[1:]
    aqs[...] = totals[:, rows:]
    ap_copy = send(aqs, aqr, ap_sem, 0, (partner, feat))
    sent.append(ap_copy)
    ap_copy.wait_recv()
    whole = (totals[:, :rows] + aqr[...]).astype(BF)
    aq[feat] = whole[width:]
    aq_copies = [None]
    for step in range(1, n_feat):
        aq_copies.append(
            send(aq.at[feat], aq.at[feat], aq_sem, step, (dom, feat_at(step)))
        )
    grad = dot(wq_cols, whole[:width], 1, 0)
    for step in range(1, n_plane):
        gr_copies[step].wait_recv()
        kv_own = kv_own + grecv[step].astype(F32)
    grad = grad + (alive / inv_count) * dot(wkv, kv_own.astype(BF), 1, 1)
    grad = grad.reshape(n_feat, width, rows)
    part[...] = grad
    gp[...] = grad.astype(BF)
    gp_copies = [None]
    for step in range(1, n_feat):
        target = feat_at(step)
        gp_copies.append(send(gp.at[target], gpr.at[step], gp_sem, step, (dom, target)))
    sent += aq_copies[1:] + gp_copies[1:]
    for step in range(1, n_feat):
        aq_copies[step].wait_recv()
    att_full = aq[...].reshape(n_feat * width, rows)
    out_ref[:width] = (alive * dot(wo_cols, att_full, 0, 0)).astype(BF)
    total = part[feat]
    for step in range(1, n_feat):
        gp_copies[step].wait_recv()
        total = total + gpr[step].astype(F32)
    out_ref[width:] = total.astype(BF)
    for copy in sent:
        copy.wait_send()


def fused(n_dom, n_feat, node_x, cotangent, assign, part_sizes, w_query, w_key, w_value, w_out):
    rows, width = node_x.shape
    n_plane = n_dom // 2
    vmem = pl.BlockSpec(memory_space=pltpu.VMEM)
    smem = pl.BlockSpec(memory_space=pltpu.SMEM)
    pair = 2 * width

    def sems(count):
        return pltpu.SemaphoreType.DMA((2, count))

    both = pl.pallas_call(
        functools.partial(kernel, n_dom, n_feat),
        out_shape=jax.ShapeDtypeStruct((pair, rows), BF),
        in_specs=[vmem, vmem, vmem, smem, vmem, vmem, vmem, vmem],
        out_specs=vmem,
        scratch_shapes=[
            pltpu.VMEM((n_dom, width, rows), BF),
            pltpu.VMEM((n_dom, 8, rows), F32),
            pltpu.VMEM((n_feat, width, rows), BF),
            pltpu.VMEM((n_feat, width, rows), BF),
            pltpu.VMEM((n_dom, 8, rows), F32),
            pltpu.VMEM((n_plane, rows, pair), BF),
            pltpu.VMEM((2, pair, rows), BF),
            pltpu.VMEM((2, 8, 2 * rows), F32),
            pltpu.VMEM((n_plane, rows, pair), BF),
            pltpu.VMEM((n_plane, rows, pair), BF),
            pltpu.VMEM((pair, rows), F32),
            pltpu.VMEM((pair, rows), F32),
            pltpu.VMEM((n_feat, width, rows), BF),
            pltpu.VMEM((n_feat, width, rows), BF),
            pltpu.VMEM((n_feat, width, rows), F32),
            pltpu.VMEM((n_feat, width, rows), BF),
            pltpu.VMEM((n_feat, width, rows), BF),
            pltpu.VMEM((n_plane, rows, 2 * rows), F32),
            pltpu.VMEM((n_plane, rows, 2 * rows), F32),
            pltpu.VMEM((2, pair, n_plane * rows), BF),
            pltpu.VMEM((2, n_plane * rows, 2 * rows), BF),
            sems(n_dom),
            sems(n_dom),
            sems(n_feat),
            sems(n_feat),
            sems(n_dom),
            sems(n_plane),
            sems(1),
            sems(1),
            sems(n_plane),
            sems(1),
            sems(n_feat),
            sems(n_feat),
            sems(n_feat),
        ],
        compiler_params=pltpu.CompilerParams(collective_id=0, has_side_effects=True),
    )(
        node_x.T,
        cotangent.T,
        assign.reshape(1, rows),
        part_sizes,
        w_query,
        w_key,
        w_value,
        w_out,
    )
    return both[:width].T, both[width:].T


def trans_dot(left, right):
    return lax.dot_general(
        left, right, (((1,), (1,)), ((), ())), preferred_element_type=jnp.float32
    )


def inner_dot(left, right):
    return lax.dot_general(
        left, right, (((0,), (0,)), ((), ())), preferred_element_type=jnp.float32
    )


def local(node_x, cotangent, assign, part_sizes, w_query, w_key, w_value, w_out):
    row_count, head_width = node_x.shape
    inv_root = 1.0 / head_width**0.5
    offset = lax.axis_index("feat") * head_width
    wq_rows = lax.dynamic_slice_in_dim(w_query, offset, head_width, 0)
    wq_cols = lax.dynamic_slice_in_dim(w_query, offset, head_width, 1)
    wkv_cols = jnp.concatenate(
        [
            lax.dynamic_slice_in_dim(w_key, offset, head_width, 1),
            lax.dynamic_slice_in_dim(w_value, offset, head_width, 1),
        ],
        axis=1,
    )
    wo_rows = lax.dynamic_slice_in_dim(w_out, offset, head_width, 0)
    wo_cols = lax.dynamic_slice_in_dim(w_out, offset, head_width, 1)
    wk_rows = lax.dynamic_slice_in_dim(w_key, offset, head_width, 0).reshape(
        head_width, HEADS, 1, head_width
    )
    wv_rows = lax.dynamic_slice_in_dim(w_value, offset, head_width, 0).reshape(
        head_width, HEADS, 1, head_width
    )
    stacked = jnp.concatenate([wk_rows, wv_rows], axis=2).reshape(
        head_width, HEADS * 2 * head_width
    )
    stacked = jnp.transpose(stacked)
    alive_rows = (jnp.arange(row_count, dtype=jnp.int32) < part_sizes[0]).astype(jnp.float32)[
        :, None
    ]
    x_piece = lax.all_gather(node_x, "feat", axis=1, tiled=True)
    grad_piece = lax.all_gather(cotangent, "feat", axis=1, tiled=True)
    query_sum = jnp.dot(x_piece, wq_cols, preferred_element_type=jnp.float32)
    grad_sum = trans_dot(grad_piece, wo_rows)
    query = query_sum.astype(jnp.bfloat16)
    g_attended = (alive_rows * grad_sum).astype(jnp.bfloat16)
    onehot = (
        (assign[:, None] == jnp.arange(CENTROIDS, dtype=jnp.int32)[None, :]) & (alive_rows > 0.0)
    ).astype(jnp.bfloat16)
    cent_sums = inner_dot(onehot, node_x)
    counts = jnp.sum(onehot.astype(jnp.float32), axis=0)
    owned_sums, owned_counts = (
        lax.psum_scatter(cent_sums, "dom", scatter_dimension=0, tiled=True),
        lax.psum_scatter(counts, "dom", scatter_dimension=0, tiled=True),
    )
    owned_cent = (owned_sums / (owned_counts + 1.0)[:, None]).astype(jnp.bfloat16)
    owned_full = lax.all_gather(owned_cent, "feat", axis=1, tiled=True)
    owned_kv = jnp.dot(owned_full, wkv_cols, preferred_element_type=jnp.float32).astype(
        jnp.bfloat16
    )
    key_value = lax.all_gather(owned_kv, "dom", axis=0, tiled=True)
    keys = key_value[:, :head_width]
    values = key_value[:, head_width:]
    quarter = row_count // 4
    block_ids = jnp.arange(4, dtype=jnp.int32)
    live_blocks = (part_sizes[0] + quarter - 1) // quarter

    def attend_block(query_block, grad_block):
        scores = trans_dot(query_block, keys) * inv_root
        probs = jax.nn.softmax(scores, axis=1)
        probs_low = probs.astype(jnp.bfloat16)
        attended = jnp.dot(probs_low, values, preferred_element_type=jnp.float32).astype(
            jnp.bfloat16
        )
        g_probs = trans_dot(grad_block, values)
        row_delta = jnp.sum(probs * g_probs, axis=1, keepdims=True)
        g_scores = (probs * (g_probs - row_delta) * inv_root).astype(jnp.bfloat16)
        g_query = jnp.dot(g_scores, keys, preferred_element_type=jnp.float32).astype(jnp.bfloat16)
        key_grad = inner_dot(g_scores, query_block)
        value_grad = inner_dot(probs_low, grad_block)
        return (jnp.concatenate([key_grad, value_grad], axis=1), attended, g_query)

    def skip_block(query_block, grad_block):
        return (
            jnp.zeros((CENTROIDS, 2 * head_width), jnp.float32),
            jnp.zeros(query_block.shape, jnp.bfloat16),
            jnp.zeros(query_block.shape, jnp.bfloat16),
        )

    def step_block(running, block_triple):
        query_block, grad_block, active = block_triple
        kv_part, attended, g_query = lax.cond(
            active, attend_block, skip_block, query_block, grad_block
        )
        return (running + kv_part, (attended, g_query))

    start_grads = jnp.zeros((CENTROIDS, 2 * head_width), jnp.float32)
    kv_sum, outputs = lax.scan(
        step_block,
        start_grads,
        (
            query.reshape(4, quarter, head_width),
            g_attended.reshape(4, quarter, head_width),
            block_ids < live_blocks,
        ),
    )
    attended = outputs[0].reshape(row_count, head_width)
    g_query = outputs[1].reshape(row_count, head_width)
    out_wide = jnp.dot(
        lax.all_gather(attended, "feat", axis=1, tiled=True),
        wo_cols,
        preferred_element_type=jnp.float32,
    )
    result_out = (alive_rows * out_wide).astype(jnp.bfloat16)
    owned_grads = lax.psum_scatter(kv_sum, "dom", scatter_dimension=0, tiled=True).astype(
        jnp.bfloat16
    )
    owned_cent_grad = jnp.dot(
        lax.all_gather(owned_grads, "feat", axis=1, tiled=True),
        stacked,
        preferred_element_type=jnp.float32,
    )
    owned_cent_grad = owned_cent_grad / (owned_counts + 1.0)[:, None]
    cent_grad = lax.all_gather(owned_cent_grad, "dom", axis=0, tiled=True)
    from_query = trans_dot(lax.all_gather(g_query, "feat", axis=1, tiled=True), wq_rows)
    grad_x = (from_query + alive_rows * jnp.take(cent_grad, assign, axis=0)).astype(jnp.bfloat16)
    return (result_out, grad_x)


def solution(mesh):
    placed = (P("dom", "feat"), P("dom", "feat"), P("dom"), P("dom"), P(), P(), P(), P())
    n_dom, n_feat = mesh.shape["dom"], mesh.shape["feat"]

    def step(node_x, *rest):
        if n_dom % 2 == 0 and n_dom * node_x.shape[0] < CENTROIDS:
            return fused(n_dom, n_feat, node_x, *rest)
        return local(node_x, *rest)

    return jax.shard_map(
        step,
        mesh=mesh,
        in_specs=placed,
        out_specs=(P("dom", "feat"), P("dom", "feat")),
        check_vma=False,
    )
```
